512 devices in a mesh: sec: 4 (over y), row: 8 (over z_lo), col: 16 (over z_hi, x, core).
Axes of the slice: x: 4, y: 4, z: 16 (z_hi: 2, z_lo: 8; z = z_hi * 8 + z_lo), core: 2. Of those that a mesh axis runs over, the one named last changes fastest.
Arguments:
- rhs: float32 [4, 8192, 256], P('sec', ('row', 'col')), may hold values from -6 to 6
- inv_factor: float32 [4, 8192, 8192], P('sec', 'col', 'row')
- coupling: float32 [4, 8192, 8192], P('sec', 'row', 'col'), may hold values from -0.0625 to 0.0625
- pattern: int32 [4, 64, 64], P('sec', 'row', 'col'), may hold values 0 or 1
Outputs:
- solution: float32 [4, 8192, 256], P('sec', 'col')
- outgoing: float32 [4, 8192, 256], P('sec', ('row', 'col'))
The draws below stay inside these ranges and needn't reach their ends.
All inputs are finite; a program needn't handle non-finite values. No bound on the sum of `pattern` on one device may be relied on, other than what follows from the above.
Results may differ from the reference program's by a relative error of at most 0.0001.
Values sent between devices are 32-bit elements; how exact they have to be, the bound alone decides.
A program may use at most 64 MiB of HBM per device.

```python
import math
import jax
import jax.numpy as jnp
from jax import lax

S = 8192
BLK = 128
NRHS = 256
BLOCKS = 64
N_SEC = 4


def draw_inv_factor(key, part):
    shape = (N_SEC, S, S)
    noise = jax.random.normal(key, shape, jnp.float32)
    lower = jnp.tril(noise, -1) * (1.5 / math.sqrt(S))
    return lower + jnp.eye(S, dtype=jnp.float32)


def place_ends(result, key, least, top_value):
    spot = [jax.random.randint(jax.random.fold_in(key, axis), (), 0, length) for axis, length in enumerate(result.shape)]
    longest = result.shape.index(max(result.shape))
    next_to = spot[:longest] + [(spot[longest] + 1) % result.shape[longest]] + spot[longest + 1:]
    return result.at[tuple(spot)].set(least).at[tuple(next_to)].set(top_value)


def block_scale(rng, dims, shards, low, high):
    def one(position, blocks):
        heights = jax.random.uniform(jax.random.fold_in(jax.random.fold_in(rng, 6), position), (blocks,), jnp.float32, low / len(shards), high / len(shards))
        return jnp.repeat(jnp.exp(heights), dims[position] // blocks).reshape((-1,) + (1,) * (len(dims) - position - 1))

    gain = one(*shards[0])
    for cut in shards[1:]:
        gain = gain * one(*cut)
    return gain


def centred(rng, extent, deviation, reach, split=(), kind=jnp.bfloat16):
    drawn = deviation * jax.random.normal(rng, extent, jnp.float32)
    if split:
        drawn = drawn * block_scale(rng, extent, split, -0.22, 0.18)
    return jnp.clip(drawn, -reach, reach).astype(kind)


def setup_inputs(seed: int = 0) -> dict:
    key_list = jax.random.split(jax.random.key(seed), 5)
    return {
        "rhs": centred(key_list[0], (N_SEC, S, NRHS), 1.0, 6.0, ((0, 4), (1, 128)), jnp.float32),
        "inv_factor": draw_inv_factor(jax.random.fold_in(key_list[4], 71), 0),
        "coupling": centred(key_list[2], (N_SEC, S, S), S ** -0.5, 0.0625, ((0, 4), (1, 8), (2, 16)), jnp.float32),
        "pattern": place_ends((jax.random.randint(key_list[3], (N_SEC, BLOCKS, BLOCKS), 0, 20) < 17).astype(jnp.int32), jax.random.fold_in(key_list[3], 1), 0, 1),
    }


def masked_panel(coupling, pattern, section):
    occupancy = pattern[section].astype(jnp.float32)
    blocks = occupancy.shape[0]
    panel = coupling[section].reshape(blocks, BLK, blocks, BLK) * occupancy[:, None, :, None]
    return panel.reshape(S, S)


def reference(rhs, inv_factor, coupling, pattern):
    highest = lax.Precision.HIGHEST
    solved_list = []
    sends = []
    parent_rhs = rhs[N_SEC - 1]
    for section in range(N_SEC - 1):
        solved = jnp.dot(inv_factor[section], rhs[section], precision=highest, preferred_element_type=jnp.float32)
        update = jnp.dot(masked_panel(coupling, pattern, section), solved, precision=highest, preferred_element_type=jnp.float32)
        parent_rhs = parent_rhs - update
        solved_list.append(solved)
        sends.append(update)
    solved = jnp.dot(inv_factor[N_SEC - 1], parent_rhs, precision=highest, preferred_element_type=jnp.float32)
    update = jnp.dot(masked_panel(coupling, pattern, N_SEC - 1), solved, precision=highest, preferred_element_type=jnp.float32)
    solved_list.append(solved)
    sends.append(update)
    return jnp.stack(solved_list), jnp.stack(sends)
```

```python
import jax
import jax.numpy as jnp
from jax import lax
from jax.experimental import pallas as pl
from jax.experimental.pallas import tpu as pltpu
from jax.sharding import PartitionSpec as P

MESH = pl.DeviceIdType.MESH
F32 = jnp.float32
BF16 = jnp.bfloat16
CHUNK = 32
CHUNKS = 512 // CHUNK
LAG = 5


def split(v):
    high = v.astype(BF16)
    return high, (v - high.astype(F32)).astype(BF16)


def dot3(ah, al, bh, bl):
    low = jnp.dot(al, bh, preferred_element_type=F32) + jnp.dot(ah, bl, preferred_element_type=F32)
    return jnp.dot(ah, bh, preferred_element_type=F32) + low


def kernel(
    rhs, inv_hbm, cpl_hbm, pat, sol, out,
    inv_v, cpl_v, ah, al, ch, cl, xg, xh, xl, part, inb, bk, yh, yl,
    ub, cb, vb, rb, wb, pb, qb, qr, zb, ob,
    load_sem, store_sem, z0s, z0r, axs, axr, acs, acr, fs, fr, bs, br,
    cs, cr, rs, rr, ys, yr, qs, qrs, zs, zr,
):
    s, r, c = lax.axis_index("sec"), lax.axis_index("row"), lax.axis_index("col")
    zh, x, k = c // 8, (c // 2) % 4, c % 2
    is_parent = s == 3
    depth = jnp.where(r < 4, r, 7 - r)
    inward = jnp.where(r < 4, r + 1, r - 1)
    outward = jnp.clip(jnp.where(r < 4, r - 1, r + 1), 0, 7)

    def at(zz, xx, kk):
        return {"col": zz * 8 + xx * 2 + kk}

    core = at(zh, x, 1 - k)
    far = at(1 - zh, x, k)
    ring = {d: at(zh, (x + d) % 4, k) for d in (1, 2, 3)}

    def remote(src, dst, send, recv, device):
        return pltpu.make_async_remote_copy(
            src_ref=src, dst_ref=dst, send_sem=send, recv_sem=recv, device_id=device, device_id_type=MESH
        )

    load_inv = pltpu.make_async_copy(inv_hbm, inv_v, load_sem.at[0])
    load_cpl = pltpu.make_async_copy(cpl_hbm, cpl_v, load_sem.at[1])
    load_inv.start()
    load_cpl.start()

    barrier = pltpu.get_barrier_semaphore()

    def greet(device):
        pl.semaphore_signal(barrier, inc=1, device_id=device, device_id_type=MESH)

    for device in (core, far, ring[1], ring[2], ring[3], {"row": inward}):
        greet(device)

    @pl.when(depth > 0)
    def _():
        greet({"row": outward})

    @pl.when(is_parent)
    def _():
        for child in range(3):
            greet({"sec": child})

    @pl.when(jnp.logical_not(is_parent))
    def _():
        greet({"sec": 3})

    pl.semaphore_wait(barrier, 7 + jnp.where(depth > 0, 1, 0) + jnp.where(is_parent, 2, 0))

    def gather_copy(zz, d, src):
        return remote(src, xg.at[zz, x, k], axs.at[zz, d - 1], axr.at[zz, d - 1], ring[d])

    def core_copy(zz, d, src):
        return remote(src, xg.at[zz, (x + 4 - d) % 4, k], acs.at[zz, d], acr.at[zz, d], core)

    def gather_send(zz, src):
        for d in (2, 1, 3):
            gather_copy(zz, d, src).start()
        core_copy(zz, 0, src).start()

    def gather_forward(zz):
        for d in (1, 3, 2):
            piece = xg.at[zz, (x + 4 - d) % 4, k]
            gather_copy(zz, d, piece).wait_recv()
            core_copy(zz, d, piece).start()

    def z0():
        return remote(rhs, xg.at[zh, x, k], z0s, z0r, far)

    @pl.when(jnp.logical_not(is_parent))
    def _():
        z0().start()
        gather_send(zh, rhs)
        xg[zh, x, k] = rhs[...]

    load_inv.wait()

    def split_inv(i, carry):
        rows = pl.ds(pl.multiple_of(i * 64, 64), 64)
        ah[rows, :], al[rows, :] = split(inv_v[rows, :])
        return carry

    lax.fori_loop(0, 8, split_inv, 0)
    load_cpl.wait()

    def split_cpl(i, carry):
        rows = pl.ds(pl.multiple_of(i * 128, 128), 128)
        to = pl.ds(pl.multiple_of((lax.rem(i, 4) * 2 + i // 4) * 128, 128), 128)
        for j in range(4):
            cols = pl.ds(j * 128, 128)
            ch[to, cols], cl[to, cols] = split(cpl_v[rows, cols] * pat[i, j].astype(F32))
        return carry

    lax.fori_loop(0, 8, split_cpl, 0)

    @pl.when(jnp.logical_not(is_parent))
    def _():
        gather_forward(zh)
        z0().wait_recv()
        gather_send(1 - zh, xg.at[1 - zh, x, k])
        gather_forward(1 - zh)
        z0().wait_send()

    def to_parent(slot):
        return remote(wb, pb.at[slot], ys, yr.at[slot], {"sec": 3})

    def q_copy():
        return remote(qb, qr, qs, qrs, far)

    @pl.when(is_parent)
    def _():
        for child in range(3):
            to_parent(child).wait_recv()
        qb[zh] = rhs[...] - (pb[0, zh] + pb[1, zh] + pb[2, zh])
        qb[1 - zh] = -(pb[0, 1 - zh] + pb[1, 1 - zh] + pb[2, 1 - zh])
        q_copy().start()
        q_copy().wait_recv()
        for zz in range(2):
            xg[zz, x, k] = qb[zz] + qr[zz]
            gather_send(zz, xg.at[zz, x, k])
        for zz in range(2):
            gather_forward(zz)
        q_copy().wait_send()

    for zz in range(2):
        for d in range(4):
            core_copy(zz, d, xg.at[zz, x, k]).wait_recv()

    for zz in range(2):
        for xx in range(4):
            for kk in range(2):
                rows = pl.ds((zz * 8 + xx * 2 + kk) * 64, 64)
                xh[rows, :], xl[rows, :] = split(xg[zz, xx, kk])

    def solve(i, carry):
        rows = pl.ds(pl.multiple_of(i * 256, 256), 256)
        part[rows, :] = dot3(ah[rows, :], al[rows, :], xh[...], xl[...])
        return carry

    lax.fori_loop(0, 2, solve, 0)

    def rows_of(m):
        return pl.ds(pl.multiple_of(m * CHUNK, CHUNK), CHUNK)

    def in_copy(m):
        return remote(part.at[rows_of(m)], inb.at[rows_of(m)], fs.at[m], fr.at[m], {"row": inward})

    def across_copy(m):
        return remote(part.at[rows_of(m)], bk.at[rows_of(m)], fs.at[m], br.at[m], {"row": inward})

    def out_copy(m):
        return remote(bk.at[rows_of(m)], bk.at[rows_of(m)], bs.at[m], br.at[m], {"row": outward})

    def forward(m):
        @pl.when(depth > 0)
        def _():
            in_copy(m).wait_recv()
            part[rows_of(m), :] = part[rows_of(m), :] + inb[rows_of(m), :]

        @pl.when(depth < 3)
        def _():
            in_copy(m).start()

        @pl.when(depth == 3)
        def _():
            across_copy(m).start()

    def back(m):
        across_copy(m).wait_recv()

        @pl.when(depth == 3)
        def _():
            bk[rows_of(m), :] = part[rows_of(m), :] + bk[rows_of(m), :]

        @pl.when(depth > 0)
        def _():
            out_copy(m).start()

    lag = jnp.where(depth == 3, LAG, CHUNKS)

    def both(i, carry):
        @pl.when(i < CHUNKS)
        def _():
            forward(i)

        @pl.when(jnp.logical_and(i >= lag, i - lag < CHUNKS))
        def _():
            back(i - lag)

        return carry

    lax.fori_loop(0, CHUNKS + lag, both, 0)

    store = pltpu.make_async_copy(bk, sol, store_sem.at[0])
    store.start()
    yh[...], yl[...] = split(bk[...])

    def pair_copy(d):
        xx = (x + d) % 4
        return remote(ub.at[1 - k, xx], cb.at[xx], cs.at[d], cr.at[d], core)

    def pair_copy_in(d):
        return pair_copy(d)

    def sum_copy(d):
        return remote(vb.at[d - 1], rb.at[d - 1], rs.at[d - 1], rr.at[d - 1], ring[d])

    order = (2, 1, 3, 0)
    for d in order:
        xx = (x + d) % 4
        rows = pl.ds(pl.multiple_of(xx * 256, 256), 256)
        u = dot3(ch[rows, :], cl[rows, :], yh[...], yl[...])
        for zz in range(2):
            for kk in range(2):
                at_row = (zz * 2 + kk) * 64
                ub[kk, xx, zz] = u[at_row : at_row + 64]
        pair_copy(d).start()
    for d in order[:3]:
        xx = (x + d) % 4
        pair_copy_in(d).wait_recv()
        vb[d - 1] = ub[k, xx] + cb[xx]
        sum_copy(d).start()
    pair_copy_in(0).wait_recv()
    own = ub[k, x] + cb[x]
    for d in (1, 3, 2):
        sum_copy(d).wait_recv()
    wb[...] = own + (rb[0] + rb[1] + rb[2])

    @pl.when(jnp.logical_not(is_parent))
    def _():
        to_parent(s).start()

    z_copy = remote(wb.at[1 - zh], zb, zs, zr, far)
    z_copy.start()
    z_copy.wait_recv()
    ob[...] = wb[zh] + zb[...]
    store_out = pltpu.make_async_copy(ob, out, store_sem.at[1])
    store_out.start()

    z_copy.wait_send()

    @pl.when(jnp.logical_not(is_parent))
    def _():
        to_parent(s).wait_send()

    for d in (1, 2, 3):
        sum_copy(d).wait_send()
    for d in range(4):
        pair_copy(d).wait_send()
    for zz in range(2):
        for d in (1, 2, 3):
            gather_copy(zz, d, xg.at[zz, x, k]).wait_send()
        for d in range(4):
            core_copy(zz, d, xg.at[zz, x, k]).wait_send()

    def drain(m, carry):
        in_copy(m).wait_send()

        @pl.when(depth > 0)
        def _():
            out_copy(m).wait_send()

        return carry

    lax.fori_loop(0, CHUNKS, drain, 0)
    store.wait()
    store_out.wait()


def shards(rhs, inv_factor, coupling, pattern):
    dma = pltpu.SemaphoreType.DMA
    vmem = pltpu.VMEM
    any_space = pl.BlockSpec(memory_space=pl.ANY)
    solved, sent = pl.pallas_call(
        kernel,
        out_shape=(jax.ShapeDtypeStruct((512, 256), F32), jax.ShapeDtypeStruct((64, 256), F32)),
        in_specs=[
            pl.BlockSpec(memory_space=pltpu.VMEM),
            any_space,
            any_space,
            pl.BlockSpec(memory_space=pltpu.SMEM),
        ],
        out_specs=(any_space, any_space),
        scratch_shapes=[
            vmem((512, 1024), F32), vmem((1024, 512), F32),
            vmem((512, 1024), BF16), vmem((512, 1024), BF16),
            vmem((1024, 512), BF16), vmem((1024, 512), BF16),
            vmem((2, 4, 2, 64, 256), F32),
            vmem((1024, 256), BF16), vmem((1024, 256), BF16),
            vmem((512, 256), F32), vmem((512, 256), F32), vmem((512, 256), F32),
            vmem((512, 256), BF16), vmem((512, 256), BF16),
            vmem((2, 4, 2, 64, 256), F32), vmem((4, 2, 64, 256), F32),
            vmem((3, 2, 64, 256), F32), vmem((3, 2, 64, 256), F32),
            vmem((2, 64, 256), F32),
            vmem((3, 2, 64, 256), F32),
            vmem((2, 64, 256), F32), vmem((2, 64, 256), F32),
            vmem((64, 256), F32), vmem((64, 256), F32),
            dma((2,)), dma((2,)), dma, dma,
            dma((2, 3)), dma((2, 3)), dma((2, 4)), dma((2, 4)),
            dma((CHUNKS,)), dma((CHUNKS,)), dma((CHUNKS,)), dma((CHUNKS,)),
            dma((4,)), dma((4,)), dma((3,)), dma((3,)),
            dma, dma((3,)), dma, dma, dma, dma,
        ],
        compiler_params=pltpu.CompilerParams(
            collective_id=0, has_side_effects=True, vmem_limit_bytes=40 * 1024 * 1024
        ),
        name="eliminate",
    )(rhs[0], inv_factor[0], coupling[0], pattern[0])
    return solved[None], sent[None]


def solution(mesh):
    placed = (
        P("sec", ("row", "col"), None),
        P("sec", "col", "row"),
        P("sec", "row", "col"),
        P("sec", "row", "col"),
    )
    return jax.shard_map(
        shards,
        mesh=mesh,
        in_specs=placed,
        out_specs=(P("sec", "col", None), P("sec", ("row", "col"), None)),
        check_vma=False,
    )
```

```python
import jax
import jax.numpy as jnp
from jax import lax
from jax.experimental import pallas as pl
from jax.experimental.pallas import tpu as pltpu
from jax.sharding import PartitionSpec as P

MESH = pl.DeviceIdType.MESH
F32 = jnp.float32
BF16 = jnp.bfloat16
HALF = 128
CHUNK = 32
PER = 512 // CHUNK
CHUNKS = 2 * PER
LAGS = (0, CHUNKS, (3 * CHUNKS) // 4, CHUNKS // 4)
SENT = PER + PER // 2


def split(v):
    high = v.astype(BF16)
    return high, (v - high.astype(F32)).astype(BF16)


def product(ah, al, b):
    wide = jnp.dot(ah, b, preferred_element_type=F32)
    low = jnp.dot(al, b[:, :HALF], preferred_element_type=F32)
    return wide[:, :HALF] + (wide[:, HALF:] + low)


def kernel(
    rhs, inv_hbm, cpl_hbm, pat, sol, out,
    inv_v, cpl_v, ah, al, ch, cl, xg, xs, part, inb, bk, yv,
    ub, cb, vb, rb, wb, pb, qb, qr, zb, ob,
    load_sem, store_sem, z0s, z0r, axs, axr, acs, acr, fs, fr, bs, br,
    cs, cr, rs, rr, ys, yr, qs, qrs, zs, zr,
):
    s, r, c = lax.axis_index("sec"), lax.axis_index("row"), lax.axis_index("col")
    zh, x, k = c // 8, (c // 2) % 4, c % 2
    is_parent = s == 3
    is_child = s < 3
    depth = jnp.where(r < 4, r, 7 - r)
    inward = jnp.where(r < 4, r + 1, r - 1)
    outward = jnp.clip(jnp.where(r < 4, r - 1, r + 1), 0, 7)

    def at(zz, xx, kk):
        return {"col": zz * 8 + xx * 2 + kk}

    core = at(zh, x, 1 - k)
    far = at(1 - zh, x, k)
    ring = {d: at(zh, (x + d) % 4, k) for d in (1, 2, 3)}

    def remote(src, dst, send, recv, device):
        return pltpu.make_async_remote_copy(
            src_ref=src, dst_ref=dst, send_sem=send, recv_sem=recv, device_id=device, device_id_type=MESH
        )

    load_inv = pltpu.make_async_copy(inv_hbm, inv_v, load_sem.at[0])
    load_cpl = pltpu.make_async_copy(cpl_hbm, cpl_v, load_sem.at[1])
    load_inv.start()
    load_cpl.start()

    barrier = pltpu.get_barrier_semaphore()

    def greet(device):
        pl.semaphore_signal(barrier, inc=1, device_id=device, device_id_type=MESH)

    for device in (far, ring[2], ring[1], ring[3], {"row": inward}, core):
        greet(device)

    @pl.when(depth > 0)
    def _():
        greet({"row": outward})

    @pl.when(is_parent)
    def _():
        for child in range(3):
            greet({"sec": child})

    @pl.when(is_child)
    def _():
        greet({"sec": 3})

    load_inv.wait()

    def split_inv(i, carry):
        rows = pl.ds(pl.multiple_of(i * 64, 64), 64)
        ah[rows, :], al[rows, :] = split(inv_v[rows, :])
        return carry

    lax.fori_loop(0, 8, split_inv, 0)
    load_cpl.wait()

    def split_cpl(i, carry):
        rows = pl.ds(pl.multiple_of(i * 128, 128), 128)
        to = pl.ds(pl.multiple_of((lax.rem(i, 4) * 2 + i // 4) * 128, 128), 128)
        for j in range(4):
            cols = pl.ds(j * 128, 128)
            ch[to, cols], cl[to, cols] = split(cpl_v[rows, cols] * pat[j, i].astype(F32))
        return carry

    lax.fori_loop(0, 8, split_cpl, 0)

    pl.semaphore_wait(barrier, 7 + jnp.where(depth > 0, 1, 0) + jnp.where(is_parent, 2, 0))

    def half(h):
        return pl.ds(h * HALF, HALF)

    def gather_copy(h, zz, d, src):
        return remote(src, xg.at[h, zz, x, k], axs.at[h, zz, d - 1], axr.at[h, zz, d - 1], ring[d])

    def core_copy(h, zz, d, src):
        return remote(src, xg.at[h, zz, (x + 4 - d) % 4, k], acs.at[h, zz, d], acr.at[h, zz, d], core)

    def gather_send(h, zz, src):
        for d in (2, 1, 3):
            gather_copy(h, zz, d, src).start()
        core_copy(h, zz, 0, src).start()

    def gather_forward(h, zz):
        for d in (1, 3, 2):
            piece = xg.at[h, zz, (x + 4 - d) % 4, k]
            gather_copy(h, zz, d, piece).wait_recv()
            core_copy(h, zz, d, piece).start()

    def z0(h):
        return remote(rhs.at[:, half(h)], xg.at[h, zh, x, k], z0s.at[h], z0r.at[h], far)

    def to_parent(h, slot):
        return remote(wb.at[h], pb.at[h, slot], ys.at[h], yr.at[h, slot], {"sec": 3})

    def q_copy(h, zz):
        return remote(qb.at[h, zz], qr.at[h, zz], qs.at[h, zz], qrs.at[h, zz], far)

    def q_send(h):
        for child in range(3):
            to_parent(h, child).wait_recv()
        for zz in range(2):
            mine = jnp.where(zh == zz, rhs[:, half(h)], 0.0)
            qb[h, zz] = mine - (pb[h, 0, zz] + pb[h, 1, zz] + pb[h, 2, zz])
            q_copy(h, zz).start()

    def q_arrive(h, zz):
        q_copy(h, zz).wait_recv()
        xg[h, zz, x, k] = qb[h, zz] + qr[h, zz]
        gather_send(h, zz, xg.at[h, zz, x, k])

    @pl.when(is_child)
    def _():
        for h in range(2):
            z0(h).start()
        for h in range(2):
            gather_send(h, zh, rhs.at[:, half(h)])
            xg[h, zh, x, k] = rhs[:, half(h)]
        for h in range(2):
            gather_forward(h, zh)
        for h in range(2):
            z0(h).wait_recv()
            gather_send(h, 1 - zh, xg.at[h, 1 - zh, x, k])
        gather_forward(0, 1 - zh)

    @pl.when(is_parent)
    def _():
        q_send(0)
        q_send(1)
        q_arrive(0, 0)
        q_arrive(0, 1)
        q_arrive(1, 0)
        gather_forward(0, 0)
        gather_forward(0, 1)

    def rows_of(m):
        return pl.ds(pl.multiple_of(m * CHUNK, CHUNK), CHUNK)

    def in_copy(m):
        return remote(part.at[rows_of(m)], inb.at[rows_of(m)], fs.at[m], fr.at[m], {"row": inward})

    def across_copy(m):
        return remote(part.at[rows_of(m)], bk.at[rows_of(m)], fs.at[m], br.at[m], {"row": inward})

    def out_copy(m):
        return remote(bk.at[rows_of(m)], bk.at[rows_of(m)], bs.at[m], br.at[m], {"row": outward})

    def solve(h):
        for zz in range(2):
            for d in range(4):
                core_copy(h, zz, d, xg.at[h, zz, x, k]).wait_recv()
        for zz in range(2):
            for xx in range(4):
                for kk in range(2):
                    rows = pl.ds((zz * 8 + xx * 2 + kk) * 64, 64)
                    xs[h, rows, :HALF], xs[h, rows, HALF:] = split(xg[h, zz, xx, kk])
        for i in range(2):
            rows = pl.ds(i * 256, 256)
            part[pl.ds(h * 512 + i * 256, 256), :] = product(ah[rows, :], al[rows, :], xs[h])

        @pl.when(depth == 0)
        def _():
            def send(m, carry):
                in_copy(m).start()
                return carry

            lax.fori_loop(h * PER, (h + 1) * PER, send, 0)

    solve(0)

    @pl.when(is_child)
    def _():
        gather_forward(1, 1 - zh)

    @pl.when(is_parent)
    def _():
        q_arrive(1, 1)
        gather_forward(1, 0)
        gather_forward(1, 1)

    solve(1)

    def forward(m):
        in_copy(m).wait_recv()
        part[rows_of(m), :] = part[rows_of(m), :] + inb[rows_of(m), :]

        @pl.when(depth < 3)
        def _():
            in_copy(m).start()

        @pl.when(depth == 3)
        def _():
            across_copy(m).start()

    def back(m):
        across_copy(m).wait_recv()

        @pl.when(depth == 3)
        def _():
            bk[rows_of(m), :] = part[rows_of(m), :] + bk[rows_of(m), :]

        @pl.when(depth > 0)
        def _():
            out_copy(m).start()

    order = (2, 1, 3, 0)

    def pair_copy(h, d):
        xx = (x + d) % 4
        return remote(ub.at[h, 1 - k, xx], cb.at[h, xx], cs.at[h, d], cr.at[h, d], core)

    def sum_copy(h, d):
        return remote(vb.at[h, d - 1], rb.at[h, d - 1], rs.at[h, d - 1], rr.at[h, d - 1], ring[d])

    def store(h):
        return pltpu.make_async_copy(bk.at[pl.ds(h * 512, 512)], sol.at[:, half(h)], store_sem.at[h])

    def apply(h):
        store(h).start()
        for i in range(2):
            rows = pl.ds(i * 256, 256)
            yv[h, rows, :HALF], yv[h, rows, HALF:] = split(bk[pl.ds(h * 512 + i * 256, 256), :])
        for d in order:
            xx = (x + d) % 4
            rows = pl.ds(pl.multiple_of(xx * 256, 256), 256)
            u = product(ch[rows, :], cl[rows, :], yv[h])
            for zz in range(2):
                for kk in range(2):
                    at_row = (zz * 2 + kk) * 64
                    ub[h, kk, xx, zz] = u[at_row : at_row + 64]
            pair_copy(h, d).start()

    def sum_send(h):
        for d in order[:3]:
            xx = (x + d) % 4
            pair_copy(h, d).wait_recv()
            vb[h, d - 1] = ub[h, k, xx] + cb[h, xx]
            sum_copy(h, d).start()

    def z_copy(h):
        return remote(wb.at[h, 1 - zh], zb.at[h], zs.at[h], zr.at[h], far)

    def sum_finish(h):
        pair_copy(h, 0).wait_recv()
        own = ub[h, k, x] + cb[h, x]
        for d in (1, 3, 2):
            sum_copy(h, d).wait_recv()
        wb[h] = own + (rb[h, 0] + rb[h, 1] + rb[h, 2])

        @pl.when(is_child)
        def _():
            to_parent(h, s).start()

        z_copy(h).start()

    lag = jnp.where(depth == 3, LAGS[3], jnp.where(depth == 2, LAGS[2], jnp.where(depth == 1, LAGS[1], LAGS[0])))

    def both(i, carry):
        j = i - lag

        @pl.when(jnp.logical_and(i < CHUNKS, depth > 0))
        def _():
            forward(i)

        @pl.when(j >= 0)
        def _():
            back(j)

        @pl.when(j == PER - 1)
        def _():
            apply(0)

        @pl.when(j == SENT - 1)
        def _():
            sum_send(0)

        return carry

    lax.fori_loop(0, CHUNKS + lag, both, 0)

    apply(1)
    sum_finish(0)
    sum_send(1)
    sum_finish(1)
    for h in range(2):
        z_copy(h).wait_recv()
        ob[:, half(h)] = wb[h, zh] + zb[h]
    store_out = pltpu.make_async_copy(ob, out, store_sem.at[2])
    store_out.start()

    for h in range(2):
        z_copy(h).wait_send()

        @pl.when(is_child)
        def _():
            to_parent(h, s).wait_send()
            z0(h).wait_send()

        @pl.when(is_parent)
        def _():
            for zz in range(2):
                q_copy(h, zz).wait_send()

        for d in (1, 2, 3):
            sum_copy(h, d).wait_send()
        for d in range(4):
            pair_copy(h, d).wait_send()
        for zz in range(2):
            for d in (1, 2, 3):
                gather_copy(h, zz, d, xg.at[h, zz, x, k]).wait_send()
            for d in range(4):
                core_copy(h, zz, d, xg.at[h, zz, x, k]).wait_send()

    def drain(m, carry):
        in_copy(m).wait_send()

        @pl.when(depth > 0)
        def _():
            out_copy(m).wait_send()

        return carry

    lax.fori_loop(0, CHUNKS, drain, 0)
    store(0).wait()
    store(1).wait()
    store_out.wait()


def shards(rhs, inv_factor, coupling, pattern):
    dma = pltpu.SemaphoreType.DMA
    vmem = pltpu.VMEM
    hbm = pl.BlockSpec(memory_space=pltpu.HBM)
    solved, sent = pl.pallas_call(
        kernel,
        out_shape=(jax.ShapeDtypeStruct((512, 256), F32), jax.ShapeDtypeStruct((64, 256), F32)),
        in_specs=[
            pl.BlockSpec(memory_space=pltpu.VMEM),
            hbm,
            hbm,
            pl.BlockSpec(memory_space=pltpu.SMEM),
        ],
        out_specs=(hbm, hbm),
        scratch_shapes=[
            vmem((512, 1024), F32), vmem((1024, 512), F32),
            vmem((512, 1024), BF16), vmem((512, 1024), BF16),
            vmem((1024, 512), BF16), vmem((1024, 512), BF16),
            vmem((2, 2, 4, 2, 64, HALF), F32),
            vmem((2, 1024, 2 * HALF), BF16),
            vmem((1024, HALF), F32), vmem((1024, HALF), F32), vmem((1024, HALF), F32),
            vmem((2, 512, 2 * HALF), BF16),
            vmem((2, 2, 4, 2, 64, HALF), F32), vmem((2, 4, 2, 64, HALF), F32),
            vmem((2, 3, 2, 64, HALF), F32), vmem((2, 3, 2, 64, HALF), F32),
            vmem((2, 2, 64, HALF), F32),
            vmem((2, 3, 2, 64, HALF), F32),
            vmem((2, 2, 64, HALF), F32), vmem((2, 2, 64, HALF), F32),
            vmem((2, 64, HALF), F32), vmem((64, 256), F32),
            dma((2,)), dma((3,)), dma((2,)), dma((2,)),
            dma((2, 2, 3)), dma((2, 2, 3)), dma((2, 2, 4)), dma((2, 2, 4)),
            dma((CHUNKS,)), dma((CHUNKS,)), dma((CHUNKS,)), dma((CHUNKS,)),
            dma((2, 4)), dma((2, 4)), dma((2, 3)), dma((2, 3)),
            dma((2,)), dma((2, 3)), dma((2, 2)), dma((2, 2)), dma((2,)), dma((2,)),
        ],
        compiler_params=pltpu.CompilerParams(
            collective_id=0, has_side_effects=True, vmem_limit_bytes=67_000_000
        ),
        name="eliminate",
    )(rhs[0], inv_factor[0], coupling[0], pattern[0].T)
    return solved[None], sent[None]


def solution(mesh):
    placed = (
        P("sec", ("row", "col"), None),
        P("sec", "col", "row"),
        P("sec", "row", "col"),
        P("sec", "row", "col"),
    )
    return jax.shard_map(
        shards,
        mesh=mesh,
        in_specs=placed,
        out_specs=(P("sec", "col", None), P("sec", ("row", "col"), None)),
        check_vma=False,
    )
```

```python
import jax
import jax.numpy as jnp
from jax import lax
from jax.experimental import pallas as pl
from jax.experimental.pallas import tpu as pltpu
from jax.sharding import PartitionSpec as P

MESH = pl.DeviceIdType.MESH
F32 = jnp.float32
BF16 = jnp.bfloat16
HALF = 128
CHUNK = 32
PER = 512 // CHUNK
CHUNKS = 2 * PER
SENT = PER + 8
LAGS = (0, CHUNKS, (3 * CHUNKS) // 4, CHUNKS // 4)


def split(v):
    high = v.astype(BF16)
    return high, (v - high.astype(F32)).astype(BF16)


def product(ah, al, b):
    wide = jnp.dot(ah, b, preferred_element_type=F32)
    low = jnp.dot(al, b[:, :HALF], preferred_element_type=F32)
    return wide[:, :HALF] + (wide[:, HALF:] + low)


def kernel(
    rhs_hbm, inv_hbm, cpl_hbm, pat_hbm, sol, out,
    pat, rhs, inv_v, cpl_v, ah, al, ch, cl, xg, xs, part, inb, bk, yv,
    ub, cb, vb, rb, wb, pb, qb, qr, zb, ob,
    load_sem, store_sem, z0s, z0r, axs, axr, acs, acr, fs, fr, bs, br,
    cs, cr, rs, rr, ys, yr, qs, qrs, zs, zr,
):
    s, r, c = lax.axis_index("sec"), lax.axis_index("row"), lax.axis_index("col")
    zh, x, k = c // 8, (c // 2) % 4, c % 2
    is_parent = s == 3
    is_child = s < 3
    depth = jnp.where(r < 4, r, 7 - r)
    inward = jnp.where(r < 4, r + 1, r - 1)
    outward = jnp.clip(jnp.where(r < 4, r - 1, r + 1), 0, 7)

    def at(zz, xx, kk):
        return {"col": zz * 8 + xx * 2 + kk}

    core = at(zh, x, 1 - k)
    far = at(1 - zh, x, k)
    ring = {d: at(zh, (x + d) % 4, k) for d in (1, 2, 3)}

    def remote(src, dst, send, recv, device):
        return pltpu.make_async_remote_copy(
            src_ref=src, dst_ref=dst, send_sem=send, recv_sem=recv, device_id=device, device_id_type=MESH
        )

    load_rhs = pltpu.make_async_copy(rhs_hbm, rhs, load_sem.at[2])
    load_pat = pltpu.make_async_copy(pat_hbm, pat, load_sem.at[3])
    load_inv = pltpu.make_async_copy(inv_hbm, inv_v, load_sem.at[0])
    load_cpl = pltpu.make_async_copy(cpl_hbm, cpl_v, load_sem.at[1])
    barrier = pltpu.get_barrier_semaphore()

    def greet(device):
        pl.semaphore_signal(barrier, inc=1, device_id=device, device_id_type=MESH)

    for device in (far, ring[2], ring[1], ring[3], {"row": inward}, core):
        greet(device)

    @pl.when(depth > 0)
    def _():
        greet({"row": outward})

    @pl.when(is_parent)
    def _():
        for child in range(3):
            greet({"sec": child})

    @pl.when(is_child)
    def _():
        greet({"sec": 3})

    load_rhs.start()
    load_pat.start()
    load_inv.start()
    load_cpl.start()
    load_rhs.wait()
    pl.semaphore_wait(barrier, 7 + jnp.where(depth > 0, 1, 0) + jnp.where(is_parent, 2, 0))

    def half(h):
        return pl.ds(h * HALF, HALF)

    def gather_copy(h, zz, d, src):
        return remote(src, xg.at[h, zz, x, k], axs.at[h, zz, d - 1], axr.at[h, zz, d - 1], ring[d])

    def core_copy(h, zz, d, src):
        return remote(src, xg.at[h, zz, (x + 4 - d) % 4, k], acs.at[h, zz, d], acr.at[h, zz, d], core)

    def gather_send(h, zz, src):
        for d in (2, 1, 3):
            gather_copy(h, zz, d, src).start()
        core_copy(h, zz, 0, src).start()

    def gather_forward(h, zz):
        for d in (1, 3, 2):
            piece = xg.at[h, zz, (x + 4 - d) % 4, k]
            gather_copy(h, zz, d, piece).wait_recv()
            core_copy(h, zz, d, piece).start()

    def z0(h):
        return remote(rhs.at[:, half(h)], xg.at[h, zh, x, k], z0s.at[h], z0r.at[h], far)

    def to_parent(h, slot):
        return remote(wb.at[h], pb.at[h, slot], ys.at[h], yr.at[h, slot], {"sec": 3})

    def q_copy(h, zz):
        return remote(qb.at[h, zz], qr.at[h, zz], qs.at[h, zz], qrs.at[h, zz], far)

    def q_send(h):
        for child in range(3):
            to_parent(h, child).wait_recv()
        for zz in range(2):
            mine = jnp.where(zh == zz, rhs[:, half(h)], 0.0)
            qb[h, zz] = mine - (pb[h, 0, zz] + pb[h, 1, zz] + pb[h, 2, zz])
            q_copy(h, zz).start()

    def q_arrive(h, zz):
        q_copy(h, zz).wait_recv()
        xg[h, zz, x, k] = qb[h, zz] + qr[h, zz]
        gather_send(h, zz, xg.at[h, zz, x, k])

    @pl.when(is_child)
    def _():
        for h in range(2):
            z0(h).start()
        for h in range(2):
            gather_send(h, zh, rhs.at[:, half(h)])
            xg[h, zh, x, k] = rhs[:, half(h)]

    load_inv.wait()

    def split_inv(i, carry):
        rows = pl.ds(pl.multiple_of(i * 64, 64), 64)
        ah[rows, :], al[rows, :] = split(inv_v[rows, :])
        return carry

    lax.fori_loop(0, 8, split_inv, 0)
    load_cpl.wait()
    load_pat.wait()

    def split_cpl(i, carry):
        rows = pl.ds(pl.multiple_of(i * 128, 128), 128)
        to = pl.ds(pl.multiple_of((lax.rem(i, 4) * 2 + i // 4) * 128, 128), 128)
        for j in range(4):
            cols = pl.ds(j * 128, 128)
            ch[to, cols], cl[to, cols] = split(cpl_v[rows, cols] * pat[j, i].astype(F32))
        return carry

    lax.fori_loop(0, 8, split_cpl, 0)

    @pl.when(is_child)
    def _():
        for h in range(2):
            gather_forward(h, zh)
        for h in range(2):
            z0(h).wait_recv()
            gather_send(h, 1 - zh, xg.at[h, 1 - zh, x, k])
        gather_forward(0, 1 - zh)

    @pl.when(is_parent)
    def _():
        q_send(0)
        q_send(1)
        q_arrive(0, 0)
        q_arrive(0, 1)
        gather_forward(0, 0)
        gather_forward(0, 1)
        q_arrive(1, 0)

    def rows_of(m):
        return pl.ds(pl.multiple_of(m * CHUNK, CHUNK), CHUNK)

    def in_copy(m):
        return remote(part.at[rows_of(m)], inb.at[rows_of(m)], fs.at[m], fr.at[m], {"row": inward})

    def across_copy(m):
        return remote(part.at[rows_of(m)], bk.at[rows_of(m)], fs.at[m], br.at[m], {"row": inward})

    def out_copy(m):
        return remote(bk.at[rows_of(m)], bk.at[rows_of(m)], bs.at[m], br.at[m], {"row": outward})

    def solve(h):
        for zz in range(2):
            for d in range(4):
                core_copy(h, zz, d, xg.at[h, zz, x, k]).wait_recv()
        for zz in range(2):
            for xx in range(4):
                for kk in range(2):
                    rows = pl.ds((zz * 8 + xx * 2 + kk) * 64, 64)
                    xs[h, rows, :HALF], xs[h, rows, HALF:] = split(xg[h, zz, xx, kk])
        for i in range(2):
            rows = pl.ds(i * 256, 256)
            part[pl.ds(h * 512 + i * 256, 256), :] = product(ah[rows, :], al[rows, :], xs[h])

        @pl.when(depth == 0)
        def _():
            def send(m, carry):
                in_copy(m).start()
                return carry

            lax.fori_loop(h * PER, (h + 1) * PER, send, 0)

    solve(0)

    @pl.when(is_child)
    def _():
        gather_forward(1, 1 - zh)

    @pl.when(is_parent)
    def _():
        q_arrive(1, 1)
        gather_forward(1, 0)
        gather_forward(1, 1)

    solve(1)

    def forward(m):
        in_copy(m).wait_recv()
        part[rows_of(m), :] = part[rows_of(m), :] + inb[rows_of(m), :]

        @pl.when(depth < 3)
        def _():
            in_copy(m).start()

        @pl.when(depth == 3)
        def _():
            across_copy(m).start()

    def back(m):
        across_copy(m).wait_recv()

        @pl.when(depth == 3)
        def _():
            bk[rows_of(m), :] = part[rows_of(m), :] + bk[rows_of(m), :]

        @pl.when(depth > 0)
        def _():
            out_copy(m).start()

    order = (2, 1, 3, 0)

    def pair_copy(h, d):
        xx = (x + d) % 4
        return remote(ub.at[h, 1 - k, xx], cb.at[h, xx], cs.at[h, d], cr.at[h, d], core)

    def sum_copy(h, d):
        return remote(vb.at[h, d - 1], rb.at[h, d - 1], rs.at[h, d - 1], rr.at[h, d - 1], ring[d])

    def store(h):
        return pltpu.make_async_copy(bk.at[pl.ds(h * 512, 512)], sol.at[:, half(h)], store_sem.at[h])

    def apply(h):
        store(h).start()
        for i in range(2):
            rows = pl.ds(i * 256, 256)
            yv[h, rows, :HALF], yv[h, rows, HALF:] = split(bk[pl.ds(h * 512 + i * 256, 256), :])
        for d in order:
            xx = (x + d) % 4
            rows = pl.ds(pl.multiple_of(xx * 256, 256), 256)
            u = product(ch[rows, :], cl[rows, :], yv[h])
            for zz in range(2):
                for kk in range(2):
                    at_row = (zz * 2 + kk) * 64
                    ub[h, kk, xx, zz] = u[at_row : at_row + 64]
            pair_copy(h, d).start()

    def sum_send(h):
        for d in order[:3]:
            xx = (x + d) % 4
            pair_copy(h, d).wait_recv()
            vb[h, d - 1] = ub[h, k, xx] + cb[h, xx]
            sum_copy(h, d).start()

    def z_copy(h):
        return remote(wb.at[h, 1 - zh], zb.at[h], zs.at[h], zr.at[h], far)

    def sum_finish(h):
        pair_copy(h, 0).wait_recv()
        own = ub[h, k, x] + cb[h, x]
        for d in (1, 3, 2):
            sum_copy(h, d).wait_recv()
        wb[h] = own + (rb[h, 0] + rb[h, 1] + rb[h, 2])

        @pl.when(is_child)
        def _():
            to_parent(h, s).start()

        z_copy(h).start()

    lag = jnp.where(depth == 3, LAGS[3], jnp.where(depth == 2, LAGS[2], jnp.where(depth == 1, LAGS[1], LAGS[0])))

    def both(i, carry):
        j = i - lag

        @pl.when(jnp.logical_and(i < CHUNKS, depth > 0))
        def _():
            forward(i)

        @pl.when(j >= 0)
        def _():
            back(j)

        @pl.when(j == PER - 1)
        def _():
            apply(0)

        @pl.when(j == SENT - 1)
        def _():
            sum_send(0)

        return carry

    lax.fori_loop(0, CHUNKS + lag, both, 0)

    apply(1)
    sum_finish(0)
    sum_send(1)
    sum_finish(1)
    for h in range(2):
        z_copy(h).wait_recv()
        ob[:, half(h)] = wb[h, zh] + zb[h]
    store_out = pltpu.make_async_copy(ob, out, store_sem.at[2])
    store_out.start()

    for h in range(2):
        z_copy(h).wait_send()

        @pl.when(is_child)
        def _():
            to_parent(h, s).wait_send()
            z0(h).wait_send()

        @pl.when(is_parent)
        def _():
            for zz in range(2):
                q_copy(h, zz).wait_send()

        for d in (1, 2, 3):
            sum_copy(h, d).wait_send()
        for d in range(4):
            pair_copy(h, d).wait_send()
        for zz in range(2):
            for d in (1, 2, 3):
                gather_copy(h, zz, d, xg.at[h, zz, x, k]).wait_send()
            for d in range(4):
                core_copy(h, zz, d, xg.at[h, zz, x, k]).wait_send()

    def drain(m, carry):
        in_copy(m).wait_send()

        @pl.when(depth > 0)
        def _():
            out_copy(m).wait_send()

        return carry

    lax.fori_loop(0, CHUNKS, drain, 0)
    store(0).wait()
    store(1).wait()
    store_out.wait()


def pass_on(solved_hbm, sent_hbm, sol, out, solved, sent, in_sem, out_sem):
    parts = [(solved_hbm.at[pl.ds(i * 128, 128)], solved.at[pl.ds(i * 128, 128)], sol.at[pl.ds(i * 128, 128)]) for i in range(4)]
    parts.append((sent_hbm, sent, out))
    reads = [pltpu.make_async_copy(a, b, in_sem.at[i]) for i, (a, b, _) in enumerate(parts)]
    writes = [pltpu.make_async_copy(b, d, out_sem.at[i]) for i, (_, b, d) in enumerate(parts)]
    for read in reads:
        read.start()
    for read, write in zip(reads, writes):
        read.wait()
        write.start()
    for write in writes:
        write.wait()


def shards(rhs, inv_factor, coupling, pattern):
    dma = pltpu.SemaphoreType.DMA
    vmem = pltpu.VMEM
    hbm = pl.BlockSpec(memory_space=pltpu.HBM)
    solved, sent = pl.pallas_call(
        kernel,
        out_shape=(jax.ShapeDtypeStruct((512, 256), F32), jax.ShapeDtypeStruct((64, 256), F32)),
        in_specs=[
            hbm,
            hbm,
            hbm,
            hbm,
        ],
        out_specs=(hbm, hbm),
        scratch_shapes=[
            pltpu.SMEM((4, 8), jnp.int32),
            vmem((64, 256), F32), vmem((512, 1024), F32), vmem((1024, 512), F32),
            vmem((512, 1024), BF16), vmem((512, 1024), BF16),
            vmem((1024, 512), BF16), vmem((1024, 512), BF16),
            vmem((2, 2, 4, 2, 64, HALF), F32),
            vmem((2, 1024, 2 * HALF), BF16),
            vmem((1024, HALF), F32), vmem((1024, HALF), F32), vmem((1024, HALF), F32),
            vmem((2, 512, 2 * HALF), BF16),
            vmem((2, 2, 4, 2, 64, HALF), F32), vmem((2, 4, 2, 64, HALF), F32),
            vmem((2, 3, 2, 64, HALF), F32), vmem((2, 3, 2, 64, HALF), F32),
            vmem((2, 2, 64, HALF), F32),
            vmem((2, 3, 2, 64, HALF), F32),
            vmem((2, 2, 64, HALF), F32), vmem((2, 2, 64, HALF), F32),
            vmem((2, 64, HALF), F32), vmem((64, 256), F32),
            dma((4,)), dma((3,)), dma((2,)), dma((2,)),
            dma((2, 2, 3)), dma((2, 2, 3)), dma((2, 2, 4)), dma((2, 2, 4)),
            dma((CHUNKS,)), dma((CHUNKS,)), dma((CHUNKS,)), dma((CHUNKS,)),
            dma((2, 4)), dma((2, 4)), dma((2, 3)), dma((2, 3)),
            dma((2,)), dma((2, 3)), dma((2, 2)), dma((2, 2)), dma((2,)), dma((2,)),
        ],
        compiler_params=pltpu.CompilerParams(
            collective_id=0, has_side_effects=True, vmem_limit_bytes=67_000_000
        ),
        name="eliminate",
    )(rhs[0], inv_factor[0], coupling[0], pattern[0].T)
    solved, sent = pl.pallas_call(
        pass_on,
        out_shape=(jax.ShapeDtypeStruct((512, 256), F32), jax.ShapeDtypeStruct((64, 256), F32)),
        in_specs=[hbm, hbm],
        out_specs=(hbm, hbm),
        scratch_shapes=[vmem((512, 256), F32), vmem((64, 256), F32), dma((5,)), dma((5,))],
        compiler_params=pltpu.CompilerParams(vmem_limit_bytes=67_000_000),
        name="pass_on",
    )(solved, sent)
    return solved[None], sent[None]


def solution(mesh):
    placed = (
        P("sec", ("row", "col"), None),
        P("sec", "col", "row"),
        P("sec", "row", "col"),
        P("sec", "row", "col"),
    )
    return jax.shard_map(
        shards,
        mesh=mesh,
        in_specs=placed,
        out_specs=(P("sec", "col", None), P("sec", ("row", "col"), None)),
        check_vma=False,
    )
```

```python
import jax
import jax.numpy as jnp
from jax import lax
from jax.experimental import pallas as pl
from jax.experimental.pallas import tpu as pltpu
from jax.sharding import PartitionSpec as P

MESH = pl.DeviceIdType.MESH
F32 = jnp.float32
BF16 = jnp.bfloat16
HALF = 128
CHUNK = 32
PER = 512 // CHUNK
CHUNKS = 2 * PER
SENT = PER + 8
FIRST = 3
LAGS = (0, CHUNKS, (3 * CHUNKS) // 4, CHUNKS // 4)


def split(v):
    high = v.astype(BF16)
    return high, (v - high.astype(F32)).astype(BF16)


def product(ah, al, b):
    wide = jnp.dot(ah, b, preferred_element_type=F32)
    low = jnp.dot(al, b[:, :HALF], preferred_element_type=F32)
    return wide[:, :HALF] + (wide[:, HALF:] + low)


def kernel(
    rhs_hbm, inv_hbm, cpl_hbm, pat_hbm, sol, out,
    pat, rhs, inv_v, cpl_v, ah, al, ch, cl, xg, xs, part, inb, bk, yv,
    ub, cb, vb, rb, wb, pb, qb, qr, zb, ob,
    load_sem, store_sem, z0s, z0r, axs, axr, acs, acr, fs, fr, bs, br,
    cs, cr, rs, rr, ys, yr, qs, qrs, zs, zr,
):
    s, r, c = lax.axis_index("sec"), lax.axis_index("row"), lax.axis_index("col")
    zh, x, k = c // 8, (c // 2) % 4, c % 2
    is_parent = s == 3
    is_child = s < 3
    depth = jnp.where(r < 4, r, 7 - r)
    inward = jnp.where(r < 4, r + 1, r - 1)
    outward = jnp.clip(jnp.where(r < 4, r - 1, r + 1), 0, 7)

    def at(zz, xx, kk):
        return {"col": zz * 8 + xx * 2 + kk}

    core = at(zh, x, 1 - k)
    far = at(1 - zh, x, k)
    ring = {d: at(zh, (x + d) % 4, k) for d in (1, 2, 3)}

    def remote(src, dst, send, recv, device):
        return pltpu.make_async_remote_copy(
            src_ref=src, dst_ref=dst, send_sem=send, recv_sem=recv, device_id=device, device_id_type=MESH
        )

    load_rhs = pltpu.make_async_copy(rhs_hbm, rhs, load_sem.at[2])
    load_pat = pltpu.make_async_copy(pat_hbm, pat, load_sem.at[3])
    load_inv = pltpu.make_async_copy(inv_hbm, inv_v, load_sem.at[0])
    load_cpl = pltpu.make_async_copy(cpl_hbm, cpl_v, load_sem.at[1])
    barrier = pltpu.get_barrier_semaphore()

    def greet(device):
        pl.semaphore_signal(barrier, inc=1, device_id=device, device_id_type=MESH)

    for device in (far, ring[2], ring[1], ring[3], {"row": inward}, core):
        greet(device)

    @pl.when(depth > 0)
    def _():
        greet({"row": outward})

    @pl.when(is_parent)
    def _():
        for child in range(3):
            greet({"sec": child})

    @pl.when(is_child)
    def _():
        greet({"sec": 3})

    load_rhs.start()
    load_pat.start()
    load_inv.start()
    load_cpl.start()
    load_rhs.wait()
    pl.semaphore_wait(barrier, 7 + jnp.where(depth > 0, 1, 0) + jnp.where(is_parent, 2, 0))

    def half(h):
        return pl.ds(h * HALF, HALF)

    def gather_copy(h, zz, d, src):
        return remote(src, xg.at[h, zz, x, k], axs.at[h, zz, d - 1], axr.at[h, zz, d - 1], ring[d])

    def core_copy(h, zz, d, src):
        return remote(src, xg.at[h, zz, (x + 4 - d) % 4, k], acs.at[h, zz, d], acr.at[h, zz, d], core)

    def gather_send(h, zz, src):
        for d in (2, 1, 3):
            gather_copy(h, zz, d, src).start()
        core_copy(h, zz, 0, src).start()

    def gather_forward(h, zz):
        for d in (1, 3, 2):
            piece = xg.at[h, zz, (x + 4 - d) % 4, k]
            gather_copy(h, zz, d, piece).wait_recv()
            core_copy(h, zz, d, piece).start()

    def z0(h):
        return remote(rhs.at[:, half(h)], xg.at[h, zh, x, k], z0s.at[h], z0r.at[h], far)

    def to_parent(h, slot):
        return remote(wb.at[h], pb.at[h, slot], ys.at[h], yr.at[h, slot], {"sec": 3})

    def q_copy(h, zz):
        return remote(qb.at[h, zz], qr.at[h, zz], qs.at[h, zz], qrs.at[h, zz], far)

    def q_send(h):
        for child in range(3):
            to_parent(h, child).wait_recv()
        for zz in range(2):
            mine = jnp.where(zh == zz, rhs[:, half(h)], 0.0)
            qb[h, zz] = mine - (pb[h, 0, zz] + pb[h, 1, zz] + pb[h, 2, zz])
            q_copy(h, zz).start()

    def q_arrive(h, zz):
        q_copy(h, zz).wait_recv()
        xg[h, zz, x, k] = qb[h, zz] + qr[h, zz]
        gather_send(h, zz, xg.at[h, zz, x, k])

    @pl.when(is_child)
    def _():
        z0(0).start()

        @pl.when(zh == 0)
        def _():
            z0(1).start()

        for h in range(2):
            gather_send(h, zh, rhs.at[:, half(h)])
            xg[h, zh, x, k] = rhs[:, half(h)]

    load_inv.wait()

    def split_inv(i, carry):
        rows = pl.ds(pl.multiple_of(i * 64, 64), 64)
        ah[rows, :], al[rows, :] = split(inv_v[rows, :])
        return carry

    lax.fori_loop(0, 8, split_inv, 0)
    load_cpl.wait()
    load_pat.wait()

    def split_cpl(i, carry):
        rows = pl.ds(pl.multiple_of(i * 128, 128), 128)
        to = pl.ds(pl.multiple_of((lax.rem(i, 4) * 2 + i // 4) * 128, 128), 128)
        for j in range(4):
            cols = pl.ds(j * 128, 128)
            ch[to, cols], cl[to, cols] = split(cpl_v[rows, cols] * pat[j, i].astype(F32))
        return carry

    lax.fori_loop(0, 8, split_cpl, 0)

    @pl.when(is_child)
    def _():
        for h in range(2):
            gather_forward(h, zh)

        @pl.when(zh == 1)
        def _():
            z0(1).start()

        for h in range(2):
            z0(h).wait_recv()
            gather_send(h, 1 - zh, xg.at[h, 1 - zh, x, k])
        gather_forward(0, 1 - zh)

    @pl.when(is_parent)
    def _():
        q_send(0)
        q_send(1)
        q_arrive(0, 0)
        q_arrive(0, 1)
        gather_forward(0, 0)
        gather_forward(0, 1)
        q_arrive(1, 0)

    def rows_of(m):
        return pl.ds(pl.multiple_of(m * CHUNK, CHUNK), CHUNK)

    def in_copy(m):
        return remote(part.at[rows_of(m)], inb.at[rows_of(m)], fs.at[m], fr.at[m], {"row": inward})

    def across_copy(m):
        return remote(part.at[rows_of(m)], bk.at[rows_of(m)], fs.at[m], br.at[m], {"row": inward})

    def out_copy(m):
        return remote(bk.at[rows_of(m)], bk.at[rows_of(m)], bs.at[m], br.at[m], {"row": outward})

    def solve(h):
        for zz in range(2):
            for d in range(4):
                core_copy(h, zz, d, xg.at[h, zz, x, k]).wait_recv()
        for zz in range(2):
            for xx in range(4):
                for kk in range(2):
                    rows = pl.ds((zz * 8 + xx * 2 + kk) * 64, 64)
                    xs[h, rows, :HALF], xs[h, rows, HALF:] = split(xg[h, zz, xx, kk])
        for i in range(2):
            rows = pl.ds(i * 256, 256)
            part[pl.ds(h * 512 + i * 256, 256), :] = product(ah[rows, :], al[rows, :], xs[h])

        @pl.when(depth == 0)
        def _():
            def send(m, carry):
                in_copy(m).start()
                return carry

            lax.fori_loop(h * PER, (h + 1) * PER, send, 0)

    solve(0)

    @pl.when(is_child)
    def _():
        gather_forward(1, 1 - zh)

    @pl.when(is_parent)
    def _():
        q_arrive(1, 1)
        gather_forward(1, 0)
        gather_forward(1, 1)

    solve(1)

    def forward(m):
        in_copy(m).wait_recv()
        part[rows_of(m), :] = part[rows_of(m), :] + inb[rows_of(m), :]

        @pl.when(depth < 3)
        def _():
            in_copy(m).start()

        @pl.when(depth == 3)
        def _():
            across_copy(m).start()

    def back(m):
        across_copy(m).wait_recv()

        @pl.when(depth == 3)
        def _():
            bk[rows_of(m), :] = part[rows_of(m), :] + bk[rows_of(m), :]

        @pl.when(depth > 0)
        def _():
            out_copy(m).start()

    order = (2, 1, 3, 0)

    def pair_copy(h, d):
        xx = (x + d) % 4
        return remote(ub.at[h, 1 - k, xx], cb.at[h, xx], cs.at[h, d], cr.at[h, d], core)

    def sum_copy(h, d):
        return remote(vb.at[h, d - 1], rb.at[h, d - 1], rs.at[h, d - 1], rr.at[h, d - 1], ring[d])

    def store(h):
        return pltpu.make_async_copy(bk.at[pl.ds(h * 512, 512)], sol.at[:, half(h)], store_sem.at[h])

    def apply(h):
        store(h).start()
        for i in range(2):
            rows = pl.ds(i * 256, 256)
            yv[h, rows, :HALF], yv[h, rows, HALF:] = split(bk[pl.ds(h * 512 + i * 256, 256), :])
        for d in order:
            xx = (x + d) % 4
            rows = pl.ds(pl.multiple_of(xx * 256, 256), 256)
            u = product(ch[rows, :], cl[rows, :], yv[h])
            for zz in range(2):
                for kk in range(2):
                    at_row = (zz * 2 + kk) * 64
                    ub[h, kk, xx, zz] = u[at_row : at_row + 64]
            pair_copy(h, d).start()

    def sum_send(h):
        for d in order[:3]:
            xx = (x + d) % 4
            pair_copy(h, d).wait_recv()
            vb[h, d - 1] = ub[h, k, xx] + cb[h, xx]
            sum_copy(h, d).start()

    def z_copy(h):
        return remote(wb.at[h, 1 - zh], zb.at[h], zs.at[h], zr.at[h], far)

    def sum_finish(h):
        pair_copy(h, 0).wait_recv()
        own = ub[h, k, x] + cb[h, x]
        for d in (1, 3, 2):
            sum_copy(h, d).wait_recv()
        wb[h] = own + (rb[h, 0] + rb[h, 1] + rb[h, 2])

        @pl.when(is_child)
        def _():
            to_parent(h, s).start()

        z_copy(h).start()

    early = depth < FIRST
    lag = jnp.where(depth == 3, LAGS[3], jnp.where(depth == 2, LAGS[2], jnp.where(depth == 1, LAGS[1], LAGS[0])))

    def both(i, carry):
        j = i - lag

        @pl.when(jnp.logical_and(i < CHUNKS, depth > 0))
        def _():
            forward(i)

        @pl.when(j >= 0)
        def _():
            back(j)

        @pl.when(jnp.logical_and(j == PER - 1, early))
        def _():
            apply(0)

        @pl.when(jnp.logical_and(j == SENT - 1, early))
        def _():
            sum_send(0)

        return carry

    lax.fori_loop(0, CHUNKS + lag, both, 0)

    @pl.when(jnp.logical_not(early))
    def _():
        apply(0)

    apply(1)

    @pl.when(jnp.logical_not(early))
    def _():
        sum_send(0)
        sum_send(1)

    sum_finish(0)

    @pl.when(early)
    def _():
        sum_send(1)

    sum_finish(1)
    for h in range(2):
        z_copy(h).wait_recv()
        ob[:, half(h)] = wb[h, zh] + zb[h]
    store_out = pltpu.make_async_copy(ob, out, store_sem.at[2])
    store_out.start()

    for h in range(2):
        z_copy(h).wait_send()

        @pl.when(is_child)
        def _():
            to_parent(h, s).wait_send()
            z0(h).wait_send()

        @pl.when(is_parent)
        def _():
            for zz in range(2):
                q_copy(h, zz).wait_send()

        for d in (1, 2, 3):
            sum_copy(h, d).wait_send()
        for d in range(4):
            pair_copy(h, d).wait_send()
        for zz in range(2):
            for d in (1, 2, 3):
                gather_copy(h, zz, d, xg.at[h, zz, x, k]).wait_send()
            for d in range(4):
                core_copy(h, zz, d, xg.at[h, zz, x, k]).wait_send()

    def drain(m, carry):
        in_copy(m).wait_send()

        @pl.when(depth > 0)
        def _():
            out_copy(m).wait_send()

        return carry

    lax.fori_loop(0, CHUNKS, drain, 0)
    store(0).wait()
    store(1).wait()
    store_out.wait()


def pass_on(solved_hbm, sent_hbm, sol, out, solved, sent, in_sem, out_sem):
    parts = [(solved_hbm.at[pl.ds(i * 128, 128)], solved.at[pl.ds(i * 128, 128)], sol.at[pl.ds(i * 128, 128)]) for i in range(4)]
    parts.append((sent_hbm, sent, out))
    reads = [pltpu.make_async_copy(a, b, in_sem.at[i]) for i, (a, b, _) in enumerate(parts)]
    writes = [pltpu.make_async_copy(b, d, out_sem.at[i]) for i, (_, b, d) in enumerate(parts)]
    for read in reads:
        read.start()
    for read, write in zip(reads, writes):
        read.wait()
        write.start()
    for write in writes:
        write.wait()


def shards(rhs, inv_factor, coupling, pattern):
    dma = pltpu.SemaphoreType.DMA
    vmem = pltpu.VMEM
    hbm = pl.BlockSpec(memory_space=pltpu.HBM)
    solved, sent = pl.pallas_call(
        kernel,
        out_shape=(jax.ShapeDtypeStruct((512, 256), F32), jax.ShapeDtypeStruct((64, 256), F32)),
        in_specs=[
            hbm,
            hbm,
            hbm,
            hbm,
        ],
        out_specs=(hbm, hbm),
        scratch_shapes=[
            pltpu.SMEM((4, 8), jnp.int32),
            vmem((64, 256), F32), vmem((512, 1024), F32), vmem((1024, 512), F32),
            vmem((512, 1024), BF16), vmem((512, 1024), BF16),
            vmem((1024, 512), BF16), vmem((1024, 512), BF16),
            vmem((2, 2, 4, 2, 64, HALF), F32),
            vmem((2, 1024, 2 * HALF), BF16),
            vmem((1024, HALF), F32), vmem((1024, HALF), F32), vmem((1024, HALF), F32),
            vmem((2, 512, 2 * HALF), BF16),
            vmem((2, 2, 4, 2, 64, HALF), F32), vmem((2, 4, 2, 64, HALF), F32),
            vmem((2, 3, 2, 64, HALF), F32), vmem((2, 3, 2, 64, HALF), F32),
            vmem((2, 2, 64, HALF), F32),
            vmem((2, 3, 2, 64, HALF), F32),
            vmem((2, 2, 64, HALF), F32), vmem((2, 2, 64, HALF), F32),
            vmem((2, 64, HALF), F32), vmem((64, 256), F32),
            dma((4,)), dma((3,)), dma((2,)), dma((2,)),
            dma((2, 2, 3)), dma((2, 2, 3)), dma((2, 2, 4)), dma((2, 2, 4)),
            dma((CHUNKS,)), dma((CHUNKS,)), dma((CHUNKS,)), dma((CHUNKS,)),
            dma((2, 4)), dma((2, 4)), dma((2, 3)), dma((2, 3)),
            dma((2,)), dma((2, 3)), dma((2, 2)), dma((2, 2)), dma((2,)), dma((2,)),
        ],
        compiler_params=pltpu.CompilerParams(
            collective_id=0, has_side_effects=True, vmem_limit_bytes=67_000_000
        ),
        name="eliminate",
    )(rhs[0], inv_factor[0], coupling[0], pattern[0].T)
    solved, sent = pl.pallas_call(
        pass_on,
        out_shape=(jax.ShapeDtypeStruct((512, 256), F32), jax.ShapeDtypeStruct((64, 256), F32)),
        in_specs=[hbm, hbm],
        out_specs=(hbm, hbm),
        scratch_shapes=[vmem((512, 256), F32), vmem((64, 256), F32), dma((5,)), dma((5,))],
        compiler_params=pltpu.CompilerParams(vmem_limit_bytes=67_000_000),
        name="pass_on",
    )(solved, sent)
    return solved[None], sent[None]


def solution(mesh):
    placed = (
        P("sec", ("row", "col"), None),
        P("sec", "col", "row"),
        P("sec", "row", "col"),
        P("sec", "row", "col"),
    )
    return jax.shard_map(
        shards,
        mesh=mesh,
        in_specs=placed,
        out_specs=(P("sec", "col", None), P("sec", ("row", "col"), None)),
        check_vma=False,
    )
```

```python
import jax
import jax.numpy as jnp
from jax import lax
from jax.experimental import pallas as pl
from jax.experimental.pallas import tpu as pltpu
from jax.sharding import PartitionSpec as P

MESH = pl.DeviceIdType.MESH
F32 = jnp.float32
BF16 = jnp.bfloat16
HALF = 128
CHUNK = 32
PER = 512 // CHUNK
CHUNKS = 2 * PER
SENT = PER + 8
FIRST = 3
LAGS = (0, CHUNKS, 26, 10)


def split(v):
    high = v.astype(BF16)
    return high, (v - high.astype(F32)).astype(BF16)


def product(ah, al, b):
    wide = jnp.dot(ah, b, preferred_element_type=F32)
    low = jnp.dot(al, b[:, :HALF], preferred_element_type=F32)
    return wide[:, :HALF] + (wide[:, HALF:] + low)


def kernel(
    rhs_hbm, inv_hbm, cpl_hbm, pat_hbm, sol, out,
    pat, rhs, inv_v, cpl_v, ah, al, ch, cl, xg, xs, part, inb, bk, yv,
    ub, cb, vb, rb, wb, pb, qb, qr, zb, ob,
    load_sem, store_sem, z0s, z0r, axs, axr, acs, acr, fs, fr, bs, br,
    cs, cr, rs, rr, ys, yr, qs, qrs, zs, zr,
):
    s, r, c = lax.axis_index("sec"), lax.axis_index("row"), lax.axis_index("col")
    zh, x, k = c // 8, (c // 2) % 4, c % 2
    is_parent = s == 3
    is_child = s < 3
    depth = jnp.where(r < 4, r, 7 - r)
    inward = jnp.where(r < 4, r + 1, r - 1)
    outward = jnp.clip(jnp.where(r < 4, r - 1, r + 1), 0, 7)

    def at(zz, xx, kk):
        return {"col": zz * 8 + xx * 2 + kk}

    core = at(zh, x, 1 - k)
    far = at(1 - zh, x, k)
    ring = {d: at(zh, (x + d) % 4, k) for d in (1, 2, 3)}

    def remote(src, dst, send, recv, device):
        return pltpu.make_async_remote_copy(
            src_ref=src, dst_ref=dst, send_sem=send, recv_sem=recv, device_id=device, device_id_type=MESH
        )

    load_rhs = pltpu.make_async_copy(rhs_hbm, rhs, load_sem.at[2])
    load_pat = pltpu.make_async_copy(pat_hbm, pat, load_sem.at[3])
    load_inv = pltpu.make_async_copy(inv_hbm, inv_v, load_sem.at[0])
    load_cpl = pltpu.make_async_copy(cpl_hbm, cpl_v, load_sem.at[1])
    barrier = pltpu.get_barrier_semaphore()

    def greet(device):
        pl.semaphore_signal(barrier, inc=1, device_id=device, device_id_type=MESH)

    for device in (far, ring[2], ring[1], ring[3], {"row": inward}, core):
        greet(device)

    @pl.when(depth > 0)
    def _():
        greet({"row": outward})

    @pl.when(is_parent)
    def _():
        for child in range(3):
            greet({"sec": child})

    @pl.when(is_child)
    def _():
        greet({"sec": 3})

    load_rhs.start()
    load_pat.start()
    load_inv.start()
    load_cpl.start()
    load_rhs.wait()
    pl.semaphore_wait(barrier, 7 + jnp.where(depth > 0, 1, 0) + jnp.where(is_parent, 2, 0))

    def half(h):
        return pl.ds(h * HALF, HALF)

    def gather_copy(h, zz, d, src):
        return remote(src, xg.at[h, zz, x, k], axs.at[h, zz, d - 1], axr.at[h, zz, d - 1], ring[d])

    def core_copy(h, zz, d, src):
        return remote(src, xg.at[h, zz, (x + 4 - d) % 4, k], acs.at[h, zz, d], acr.at[h, zz, d], core)

    def gather_send(h, zz, src):
        for d in (2, 1, 3):
            gather_copy(h, zz, d, src).start()
        core_copy(h, zz, 0, src).start()

    def gather_forward(h, zz):
        for d in (1, 3, 2):
            piece = xg.at[h, zz, (x + 4 - d) % 4, k]
            gather_copy(h, zz, d, piece).wait_recv()
            core_copy(h, zz, d, piece).start()

    def z0(h):
        return remote(rhs.at[:, half(h)], xg.at[h, zh, x, k], z0s.at[h], z0r.at[h], far)

    def to_parent(h, slot):
        return remote(wb.at[h], pb.at[h, slot], ys.at[h], yr.at[h, slot], {"sec": 3})

    def q_copy(h, zz):
        return remote(qb.at[h, zz], qr.at[h, zz], qs.at[h, zz], qrs.at[h, zz], far)

    def q_send(h):
        for child in range(3):
            to_parent(h, child).wait_recv()
        for zz in range(2):
            mine = jnp.where(zh == zz, rhs[:, half(h)], 0.0)
            qb[h, zz] = mine - (pb[h, 0, zz] + pb[h, 1, zz] + pb[h, 2, zz])
            q_copy(h, zz).start()

    def q_arrive(h, zz):
        q_copy(h, zz).wait_recv()
        xg[h, zz, x, k] = qb[h, zz] + qr[h, zz]
        gather_send(h, zz, xg.at[h, zz, x, k])

    @pl.when(is_child)
    def _():
        z0(0).start()

        @pl.when(zh == 0)
        def _():
            z0(1).start()

        for h in range(2):
            gather_send(h, zh, rhs.at[:, half(h)])
            xg[h, zh, x, k] = rhs[:, half(h)]

    load_inv.wait()

    def split_inv(i, carry):
        rows = pl.ds(pl.multiple_of(i * 64, 64), 64)
        ah[rows, :], al[rows, :] = split(inv_v[rows, :])
        return carry

    lax.fori_loop(0, 8, split_inv, 0)
    load_cpl.wait()
    load_pat.wait()

    def split_cpl(i, carry):
        rows = pl.ds(pl.multiple_of(i * 128, 128), 128)
        to = pl.ds(pl.multiple_of((lax.rem(i, 4) * 2 + i // 4) * 128, 128), 128)
        for j in range(4):
            cols = pl.ds(j * 128, 128)
            ch[to, cols], cl[to, cols] = split(cpl_v[rows, cols] * pat[j, i].astype(F32))
        return carry

    lax.fori_loop(0, 8, split_cpl, 0)

    @pl.when(is_child)
    def _():
        for h in range(2):
            gather_forward(h, zh)

        @pl.when(zh == 1)
        def _():
            z0(1).start()

        for h in range(2):
            z0(h).wait_recv()
            gather_send(h, 1 - zh, xg.at[h, 1 - zh, x, k])
        gather_forward(0, 1 - zh)

    @pl.when(is_parent)
    def _():
        q_send(0)
        q_send(1)
        q_arrive(0, 0)
        q_arrive(0, 1)
        gather_forward(0, 0)
        gather_forward(0, 1)
        q_arrive(1, 0)

    def rows_of(m):
        return pl.ds(pl.multiple_of(m * CHUNK, CHUNK), CHUNK)

    def in_copy(m):
        return remote(part.at[rows_of(m)], inb.at[rows_of(m)], fs.at[m], fr.at[m], {"row": inward})

    def across_copy(m):
        return remote(part.at[rows_of(m)], bk.at[rows_of(m)], fs.at[m], br.at[m], {"row": inward})

    def out_copy(m):
        return remote(bk.at[rows_of(m)], bk.at[rows_of(m)], bs.at[m], br.at[m], {"row": outward})

    def solve(h):
        for zz in range(2):
            for d in range(4):
                core_copy(h, zz, d, xg.at[h, zz, x, k]).wait_recv()
        for zz in range(2):
            for xx in range(4):
                for kk in range(2):
                    rows = pl.ds((zz * 8 + xx * 2 + kk) * 64, 64)
                    xs[h, rows, :HALF], xs[h, rows, HALF:] = split(xg[h, zz, xx, kk])
        for i in range(2):
            rows = pl.ds(i * 256, 256)
            part[pl.ds(h * 512 + i * 256, 256), :] = product(ah[rows, :], al[rows, :], xs[h])

        @pl.when(depth == 0)
        def _():
            def send(m, carry):
                in_copy(m).start()
                return carry

            lax.fori_loop(h * PER, (h + 1) * PER, send, 0)

    solve(0)

    @pl.when(is_child)
    def _():
        gather_forward(1, 1 - zh)

    @pl.when(is_parent)
    def _():
        q_arrive(1, 1)
        gather_forward(1, 0)
        gather_forward(1, 1)

    solve(1)

    def forward(m):
        in_copy(m).wait_recv()
        part[rows_of(m), :] = part[rows_of(m), :] + inb[rows_of(m), :]

        @pl.when(depth < 3)
        def _():
            in_copy(m).start()

        @pl.when(depth == 3)
        def _():
            across_copy(m).start()

    def back(m):
        across_copy(m).wait_recv()

        @pl.when(depth == 3)
        def _():
            bk[rows_of(m), :] = part[rows_of(m), :] + bk[rows_of(m), :]

        @pl.when(depth > 0)
        def _():
            out_copy(m).start()

    order = (2, 1, 3, 0)

    def pair_copy(h, d):
        xx = (x + d) % 4
        return remote(ub.at[h, 1 - k, xx], cb.at[h, xx], cs.at[h, d], cr.at[h, d], core)

    def sum_copy(h, d):
        return remote(vb.at[h, d - 1], rb.at[h, d - 1], rs.at[h, d - 1], rr.at[h, d - 1], ring[d])

    def store(h):
        return pltpu.make_async_copy(bk.at[pl.ds(h * 512, 512)], sol.at[:, half(h)], store_sem.at[h])

    def apply(h):
        store(h).start()
        for i in range(2):
            rows = pl.ds(i * 256, 256)
            yv[h, rows, :HALF], yv[h, rows, HALF:] = split(bk[pl.ds(h * 512 + i * 256, 256), :])
        for d in order:
            xx = (x + d) % 4
            rows = pl.ds(pl.multiple_of(xx * 256, 256), 256)
            u = product(ch[rows, :], cl[rows, :], yv[h])
            for zz in range(2):
                for kk in range(2):
                    at_row = (zz * 2 + kk) * 64
                    ub[h, kk, xx, zz] = u[at_row : at_row + 64]
            pair_copy(h, d).start()

    def sum_send(h):
        for d in order[:3]:
            xx = (x + d) % 4
            pair_copy(h, d).wait_recv()
            vb[h, d - 1] = ub[h, k, xx] + cb[h, xx]
            sum_copy(h, d).start()

    def z_copy(h):
        return remote(wb.at[h, 1 - zh], zb.at[h], zs.at[h], zr.at[h], far)

    def sum_finish(h):
        pair_copy(h, 0).wait_recv()
        own = ub[h, k, x] + cb[h, x]
        for d in (1, 3, 2):
            sum_copy(h, d).wait_recv()
        wb[h] = own + (rb[h, 0] + rb[h, 1] + rb[h, 2])

        @pl.when(is_child)
        def _():
            to_parent(h, s).start()

        z_copy(h).start()

    early = depth < FIRST
    lag = jnp.where(depth == 3, LAGS[3], jnp.where(depth == 2, LAGS[2], jnp.where(depth == 1, LAGS[1], LAGS[0])))

    def both(i, carry):
        j = i - lag

        @pl.when(jnp.logical_and(i < CHUNKS, depth > 0))
        def _():
            forward(i)

        @pl.when(j >= 0)
        def _():
            back(j)

        @pl.when(jnp.logical_and(j == PER - 1, early))
        def _():
            apply(0)

        @pl.when(jnp.logical_and(j == SENT - 1, early))
        def _():
            sum_send(0)

        return carry

    lax.fori_loop(0, CHUNKS + lag, both, 0)

    @pl.when(jnp.logical_not(early))
    def _():
        apply(0)

    apply(1)

    @pl.when(jnp.logical_not(early))
    def _():
        sum_send(0)
        sum_send(1)

    sum_finish(0)

    @pl.when(early)
    def _():
        sum_send(1)

    sum_finish(1)
    for h in range(2):
        z_copy(h).wait_recv()
        ob[:, half(h)] = wb[h, zh] + zb[h]
    store_out = pltpu.make_async_copy(ob, out, store_sem.at[2])
    store_out.start()

    for h in range(2):
        z_copy(h).wait_send()

        @pl.when(is_child)
        def _():
            to_parent(h, s).wait_send()
            z0(h).wait_send()

        @pl.when(is_parent)
        def _():
            for zz in range(2):
                q_copy(h, zz).wait_send()

        for d in (1, 2, 3):
            sum_copy(h, d).wait_send()
        for d in range(4):
            pair_copy(h, d).wait_send()
        for zz in range(2):
            for d in (1, 2, 3):
                gather_copy(h, zz, d, xg.at[h, zz, x, k]).wait_send()
            for d in range(4):
                core_copy(h, zz, d, xg.at[h, zz, x, k]).wait_send()

    def drain(m, carry):
        in_copy(m).wait_send()

        @pl.when(depth > 0)
        def _():
            out_copy(m).wait_send()

        return carry

    lax.fori_loop(0, CHUNKS, drain, 0)
    store(0).wait()
    store(1).wait()
    store_out.wait()


def pass_on(solved_hbm, sent_hbm, sol, out, solved, sent, in_sem, out_sem):
    parts = [(solved_hbm.at[pl.ds(i * 128, 128)], solved.at[pl.ds(i * 128, 128)], sol.at[pl.ds(i * 128, 128)]) for i in range(4)]
    parts.append((sent_hbm, sent, out))
    reads = [pltpu.make_async_copy(a, b, in_sem.at[i]) for i, (a, b, _) in enumerate(parts)]
    writes = [pltpu.make_async_copy(b, d, out_sem.at[i]) for i, (_, b, d) in enumerate(parts)]
    for read in reads:
        read.start()
    for read, write in zip(reads, writes):
        read.wait()
        write.start()
    for write in writes:
        write.wait()


def shards(rhs, inv_factor, coupling, pattern):
    dma = pltpu.SemaphoreType.DMA
    vmem = pltpu.VMEM
    hbm = pl.BlockSpec(memory_space=pltpu.HBM)
    solved, sent = pl.pallas_call(
        kernel,
        out_shape=(jax.ShapeDtypeStruct((512, 256), F32), jax.ShapeDtypeStruct((64, 256), F32)),
        in_specs=[
            hbm,
            hbm,
            hbm,
            hbm,
        ],
        out_specs=(hbm, hbm),
        scratch_shapes=[
            pltpu.SMEM((4, 8), jnp.int32),
            vmem((64, 256), F32), vmem((512, 1024), F32), vmem((1024, 512), F32),
            vmem((512, 1024), BF16), vmem((512, 1024), BF16),
            vmem((1024, 512), BF16), vmem((1024, 512), BF16),
            vmem((2, 2, 4, 2, 64, HALF), F32),
            vmem((2, 1024, 2 * HALF), BF16),
            vmem((1024, HALF), F32), vmem((1024, HALF), F32), vmem((1024, HALF), F32),
            vmem((2, 512, 2 * HALF), BF16),
            vmem((2, 2, 4, 2, 64, HALF), F32), vmem((2, 4, 2, 64, HALF), F32),
            vmem((2, 3, 2, 64, HALF), F32), vmem((2, 3, 2, 64, HALF), F32),
            vmem((2, 2, 64, HALF), F32),
            vmem((2, 3, 2, 64, HALF), F32),
            vmem((2, 2, 64, HALF), F32), vmem((2, 2, 64, HALF), F32),
            vmem((2, 64, HALF), F32), vmem((64, 256), F32),
            dma((4,)), dma((3,)), dma((2,)), dma((2,)),
            dma((2, 2, 3)), dma((2, 2, 3)), dma((2, 2, 4)), dma((2, 2, 4)),
            dma((CHUNKS,)), dma((CHUNKS,)), dma((CHUNKS,)), dma((CHUNKS,)),
            dma((2, 4)), dma((2, 4)), dma((2, 3)), dma((2, 3)),
            dma((2,)), dma((2, 3)), dma((2, 2)), dma((2, 2)), dma((2,)), dma((2,)),
        ],
        compiler_params=pltpu.CompilerParams(
            collective_id=0, has_side_effects=True, vmem_limit_bytes=67_000_000
        ),
        name="eliminate",
    )(rhs[0], inv_factor[0], coupling[0], pattern[0].T)
    solved, sent = pl.pallas_call(
        pass_on,
        out_shape=(jax.ShapeDtypeStruct((512, 256), F32), jax.ShapeDtypeStruct((64, 256), F32)),
        in_specs=[hbm, hbm],
        out_specs=(hbm, hbm),
        scratch_shapes=[vmem((512, 256), F32), vmem((64, 256), F32), dma((5,)), dma((5,))],
        compiler_params=pltpu.CompilerParams(vmem_limit_bytes=67_000_000),
        name="pass_on",
    )(solved, sent)
    return solved[None], sent[None]


def solution(mesh):
    placed = (
        P("sec", ("row", "col"), None),
        P("sec", "col", "row"),
        P("sec", "row", "col"),
        P("sec", "row", "col"),
    )
    return jax.shard_map(
        shards,
        mesh=mesh,
        in_specs=placed,
        out_specs=(P("sec", "col", None), P("sec", ("row", "col"), None)),
        check_vma=False,
    )
```
